128 devices in a mesh: row: 4 (over z_hi, core), col: 32 (over x, z_lo, y).
Axes of the slice: x: 4, y: 4, z: 4 (z_hi: 2, z_lo: 2; z = z_hi * 2 + z_lo), core: 2. Of those that a mesh axis runs over, the one named last changes fastest.
Arguments:
- right_side: float32 [131072, 128], P(('row', 'col')), may hold values from -150 to 150
- block_values: bfloat16 [64, 917504], P(None, ('row', 'col')), may hold values from -1 to 2, as said below
- block_cols: int32 [14336], P(('row', 'col')), may hold values from 0 to 511, as said below
- row_ptrs: int32 [8320], P(('row', 'col')), may hold values from 0 to 112, as said below
- precond: float32 [131072, 1024], P(('row', 'col')), may hold values from -1 to 2, as said below
Outputs:
- solution: float32 [131072, 128], P(('row', 'col'))
- residual: float32 [131072, 128], P(('row', 'col'))
The draws below stay inside these ranges and needn't reach their ends.
Inputs may be any that keep to these rules, and one draw needn't show every extreme that they name: `row_ptrs`: in each tile t the 65 pointers from index t * (65) on never fall, start at 0 and end at 112. `block_cols`: each of the 2048 block rows of A holds 7 blocks. `block_values`: with the pattern, the blocks form a symmetric matrix A. `precond`: each 1024 x 1024 block is lower triangular with a positive diagonal.
All inputs are finite; a program needn't handle non-finite values.
Results may differ from the reference program's by a relative error of at most 0.0076.
Values may be sent and summed in bfloat16 or wider, within the bound.
A program may use at most 128 MiB of HBM per device.

```python
import math
import jax
import jax.numpy as jnp
from jax import lax

BS = 64
SB = 16
RHS = 128
ITERS = 2
S = 1024
TILE_ROWS = 64
TILE_COLS = 512
CAP = 112
ELEMENTS = 2048
N = 131072
N_ROW = 4
N_COL = 32


def tile_pattern(key):
    pattern_key = jax.random.fold_in(key, 7001)
    tile_cols = N_COL * SB
    tile_rows = N_ROW * SB
    tile_count = N_ROW * N_COL
    shift_list = []
    mappings = []
    for family in range(3):
        family_shift = jax.random.randint(jax.random.fold_in(pattern_key, 50 + family), (tile_cols,), 1, N_ROW).astype(jnp.int32)
        shift_list.append(family_shift)
        rows_list = []
        for quarter_idx in range(N_ROW):
            first_fold = jax.random.fold_in(pattern_key, 100 + family * N_ROW + quarter_idx)
            second_fold = jax.random.fold_in(pattern_key, 500 + family * N_ROW + quarter_idx)
            first_perm = jax.random.permutation(first_fold, tile_cols).astype(jnp.int32)
            second_perm = jax.random.permutation(second_fold, tile_cols).astype(jnp.int32)
            first_order = jnp.argsort(family_shift * tile_cols + first_perm).astype(jnp.int32)
            second_order = jnp.argsort(family_shift * tile_cols + second_perm).astype(jnp.int32)
            mapping = jnp.zeros((tile_cols,), jnp.int32).at[first_order].set(second_order)
            rows_list.append(mapping)
        mappings.append(jnp.stack(rows_list).astype(jnp.int32))
    mappings = jnp.stack(mappings)
    inverse = jnp.argsort(mappings, axis=-1).astype(jnp.int32)
    tile_index = jnp.arange(tile_count, dtype=jnp.int32)[:, None]
    range_idx = tile_index // N_COL
    group_idx = tile_index % N_COL
    local_row = jnp.arange(tile_rows, dtype=jnp.int32)[None, :]
    full_shape = (tile_count, tile_rows)
    row_range = jnp.broadcast_to(local_row // SB, full_shape)
    within = jnp.broadcast_to(group_idx * SB + local_row % SB, full_shape)
    range_full = jnp.broadcast_to(range_idx, full_shape)
    own_global = row_range * tile_cols + within
    present = [row_range == range_full]
    columns = [within]
    owners = [own_global]
    block_kind = [jnp.zeros(full_shape, jnp.int32)]
    for family in range(3):
        row_shift = shift_list[family][within]
        present.append((row_range + row_shift) % N_ROW == range_full)
        columns.append(mappings[family][row_range, within])
        owners.append(own_global)
        block_kind.append(jnp.full(full_shape, 1 + family, jnp.int32))
    for family in range(3):
        row_shift = shift_list[family][within]
        present.append((range_full + row_shift) % N_ROW == row_range)
        back_column = inverse[family][range_full, within]
        columns.append(back_column)
        owners.append(range_full * tile_cols + back_column)
        block_kind.append(jnp.full(full_shape, 4 + family, jnp.int32))
    present = jnp.stack(present, axis=-1)
    columns = jnp.stack(columns, axis=-1).reshape(tile_count, tile_rows * 7)
    owners = jnp.stack(owners, axis=-1).reshape(tile_count, tile_rows * 7)
    block_kind = jnp.stack(block_kind, axis=-1).reshape(tile_count, tile_rows * 7)
    flat_present = present.reshape(tile_count, tile_rows * 7)
    position = jnp.arange(tile_rows * 7, dtype=jnp.int32)[None, :]
    ranking = jnp.where(flat_present, position, tile_rows * 7 + position)
    chosen = jnp.argsort(ranking, axis=1)[:, :CAP]
    columns = jnp.take_along_axis(columns, chosen, axis=1)
    owners = jnp.take_along_axis(owners, chosen, axis=1)
    block_kind = jnp.take_along_axis(block_kind, chosen, axis=1)
    counts = jnp.sum(present.astype(jnp.int32), axis=-1)
    pointers = jnp.concatenate([jnp.zeros((tile_count, 1), jnp.int32), jnp.cumsum(counts, axis=1).astype(jnp.int32)], axis=1)
    return (columns, pointers, owners, block_kind)


def draw_block_cols(key, part):
    columns, pointers, owners, block_kind = tile_pattern(key)
    return columns.reshape(-1).astype(jnp.int32)


def draw_row_ptrs(key, part):
    columns, pointers, owners, block_kind = tile_pattern(key)
    return pointers.reshape(-1).astype(jnp.int32)


def draw_block_values(key, part):
    columns, pointers, owners, block_kind = tile_pattern(key)
    owner_flat = owners.reshape(-1)
    kind_flat = block_kind.reshape(-1)
    elements = N_ROW * N_COL * SB
    family_of = jnp.where(kind_flat == 0, 3, jnp.where(kind_flat <= 3, kind_flat - 1, kind_flat - 4))
    block_code = family_of * elements + owner_flat
    value_key = jax.random.fold_in(key, 9001)

    def one_block(code_value):
        block_key = jax.random.fold_in(value_key, code_value)
        jitter = jnp.clip(jax.random.normal(block_key, (BS, BS), jnp.float32), -4.0, 4.0)
        return jitter
    jitter = jax.vmap(one_block)(block_code)
    flipped = jnp.swapaxes(jitter, 1, 2)
    spread = 0.32 / math.sqrt(7 * BS)
    identity = jnp.eye(BS, dtype=jnp.float32)[None, :, :]
    selector = kind_flat[:, None, None]
    diagonal_block = identity + spread * (jitter + flipped) / math.sqrt(2.0)
    blocks = jnp.where(selector == 0, diagonal_block, jnp.where(selector >= 4, spread * flipped, spread * jitter))
    return jnp.transpose(blocks, (1, 0, 2)).reshape(BS, -1).astype(jnp.bfloat16)


def draw_precond(key, part):
    total_rows = S * N_ROW * N_COL
    row_index = jnp.arange(total_rows, dtype=jnp.int32)[:, None] % S
    col_index = jnp.arange(S, dtype=jnp.int32)[None, :]
    first_key = jax.random.fold_in(key, 11)
    second_key = jax.random.fold_in(key, 12)
    jitter = jnp.clip(jax.random.normal(first_key, (total_rows, S), jnp.float32), -4.0, 4.0)
    diagonal = jax.random.uniform(second_key, (total_rows, 1), jnp.float32, 0.7, 1.4)
    below = col_index < row_index
    values = jnp.where(below, jitter * (0.3 / math.sqrt(S)), jnp.where(col_index == row_index, diagonal, 0.0))
    return values.astype(jnp.float32)


def draw_right_side(key, part):
    tile_count = N_ROW * N_COL
    total_rows = S * tile_count
    segment = (jnp.arange(total_rows, dtype=jnp.int32)[:, None] // S).astype(jnp.float32)
    row_level = jnp.power(10.0, jax.random.uniform(jax.random.fold_in(key, 21), (total_rows, 1), jnp.float32))
    col_level = jnp.power(10.0, jax.random.uniform(jax.random.fold_in(key, 22), (1, RHS), jnp.float32))
    rising = 1.0 + 2.0 * segment / (tile_count - 1)
    jitter = jnp.clip(jax.random.normal(jax.random.fold_in(key, 23), (total_rows, RHS), jnp.float32), -4.0, 4.0)
    return (jitter * row_level * col_level * rising / 30.0).astype(jnp.float32)


def setup_inputs(seed: int = 0) -> dict:
    streams_of = jax.random.split(jax.random.key(seed), 6)
    right_side = draw_right_side(jax.random.fold_in(streams_of[5], 71), 0)
    block_values = draw_block_values(jax.random.fold_in(streams_of[5], 71), 0)
    block_cols = draw_block_cols(jax.random.fold_in(streams_of[5], 71), 0)
    row_ptrs = draw_row_ptrs(jax.random.fold_in(streams_of[5], 71), 0)
    precond = draw_precond(jax.random.fold_in(streams_of[5], 71), 0)
    return {"right_side": right_side, "block_values": block_values, "block_cols": block_cols, "row_ptrs": row_ptrs, "precond": precond}


def precondition(vector, precond):
    tile_count = N_ROW * N_COL
    blocks = precond.reshape(tile_count, S, S)
    segments = vector.reshape(tile_count, S, RHS)
    half_step = jnp.einsum("dij,djk->dik", blocks, segments, precision=lax.Precision.HIGHEST)
    result = jnp.einsum("dji,djk->dik", blocks, half_step, precision=lax.Precision.HIGHEST)
    return result.reshape(N, RHS)


def apply_matrix(vec_half, block_values, block_cols, row_ptrs):
    tile_count = N_ROW * N_COL
    tile_blocks = jnp.transpose(block_values.reshape(BS, tile_count, CAP, BS), (1, 0, 2, 3))
    columns = block_cols.reshape(tile_count, CAP)
    pointers = row_ptrs.reshape(tile_count, TILE_ROWS + 1)
    source = vec_half.reshape(ELEMENTS, BS, RHS)
    slot_index = jnp.arange(CAP, dtype=jnp.int32)

    def one_tile(accumulated, inputs):
        blocks, column, pointer, tile_index = inputs
        range_idx = tile_index // N_COL
        group_idx = tile_index % N_COL
        local_row = jnp.sum((slot_index[:, None] >= pointer[None, 1:]).astype(jnp.int32), axis=1)
        global_row = ((local_row // SB) * N_COL + group_idx) * SB + local_row % SB
        global_col = range_idx * TILE_COLS + column
        operand = source[global_col].astype(jnp.float32)
        product = jnp.einsum("ibj,bjk->bik", blocks.astype(jnp.float32), operand)
        return accumulated.at[global_row].add(product), None

    start = jnp.zeros((ELEMENTS, BS, RHS), jnp.float32)
    result, _ = lax.scan(one_tile, start, (tile_blocks, columns, pointers, jnp.arange(tile_count, dtype=jnp.int32)))
    return result.reshape(N, RHS)


def reference(right_side, block_values, block_cols, row_ptrs, precond):
    solution = jnp.zeros_like(right_side)
    residual = right_side
    direction = right_side
    image_vec = right_side
    alpha_prev = jnp.ones((RHS,), jnp.float32)
    gamma_prev = jnp.ones((RHS,), jnp.float32)
    for iteration in range(ITERS):
        smoothed = precondition(residual, precond)
        gamma_now = jnp.sum(residual * smoothed, axis=0)
        vec_half = lax.optimization_barrier(smoothed.astype(jnp.bfloat16))
        applied = apply_matrix(vec_half, block_values, block_cols, row_ptrs)
        delta_now = jnp.sum(smoothed * applied, axis=0)
        if iteration == 0:
            alpha_now = gamma_now / delta_now
            direction = smoothed
            image_vec = applied
        else:
            beta_now = gamma_now / gamma_prev
            alpha_now = gamma_now / (delta_now - beta_now * gamma_now / alpha_prev)
            direction = smoothed + beta_now * direction
            image_vec = applied + beta_now * image_vec
        solution = solution + alpha_now * direction
        residual = residual - alpha_now * image_vec
        gamma_prev = gamma_now
        alpha_prev = alpha_now
    return solution, residual
```

```python
import heapq

import jax
import jax.numpy as jnp
from jax import lax
from jax.experimental import pallas as pl
from jax.experimental.pallas import tpu as pltpu
from jax.sharding import PartitionSpec as P

ITERS = 2
MESH = pl.DeviceIdType.MESH
RING = {"x": 4, "z": 2, "y": 4}
DIMS = ("x", "z", "y")
PARTS = ((("z", "y", "x"), 0, 512), (("z", "x", "y"), 512, 512))
LINK_RATE = 46e3 / 256
HOP = 1.7


def shifted(offset, dim, step):
    pos = DIMS.index(dim)
    changed = list(offset)
    changed[pos] = (changed[pos] + step) % RING[dim]
    return tuple(changed)


def sends_of(part, offset, stage):
    order, start, count = PARTS[part]
    half = count // 2
    out = []
    if stage >= 0 and order[stage] != "z":
        dim = order[stage]
        value = offset[DIMS.index(dim)]
        if value == 3:
            out.append((dim, 1, start, half, (part, shifted(offset, dim, -1), "p")))
        if value == 1:
            out.append((dim, -1, start + half, half, (part, shifted(offset, dim, 1), "m")))
    for later in range(stage + 1, 3):
        dim = order[later]
        out.append((dim, 1, start, count, (part, shifted(offset, dim, -1), "f")))
        if dim != "z":
            out.append((dim, -1, start, count, (part, shifted(offset, dim, 1), "f")))
    return out


def last_stage(part, offset):
    order = PARTS[part][0]
    return max(j for j in range(3) if offset[DIMS.index(order[j])] != 0)


def gather_plan():
    heap, free, ids, plan = [], {}, {}, []

    def issue(now, offset, sends):
        for dim, step, start, count, key in sends:
            link = (dim, step)
            free[link] = max(free.get(link, 0.0), now) + count / LINK_RATE
            ids[key] = len(ids)
            heapq.heappush(heap, (free[link] + HOP, ids[key], key, start, count))

    first = []
    for part in range(len(PARTS)):
        first += [(j, s) for j, s in enumerate(sends_of(part, (0, 0, 0), -1))]
    first = [s for _, s in sorted(first, key=lambda item: item[0])]
    issue(0.0, (0, 0, 0), first)
    plan.append((None, (0, 0, 0), 0, 0, first))
    halves = set()
    while heap:
        now, _, key, start, count = heapq.heappop(heap)
        part, offset, kind = key
        stage = last_stage(part, offset)
        sends = []
        if kind == "f":
            sends = sends_of(part, offset, stage)
        elif (part, offset) in halves:
            sends = sends_of(part, offset, stage)
        else:
            halves.add((part, offset))
        issue(now, offset, sends)
        plan.append((key, offset, start, count, sends))
    return plan, ids


PLAN, COPY_IDS = gather_plan()
COPIES = len(COPY_IDS)


def position():
    row = lax.axis_index("row")
    col = lax.axis_index("col")
    return {
        "h": row // 2, "core": row % 2,
        "x": col // 8, "z": (col // 4) % 2, "y": col % 4,
    }


def device_at(pos):
    return (pos["h"] * 2 + pos["core"], (pos["x"] * 2 + pos["z"]) * 4 + pos["y"])


def col_at(pos, offset):
    x, z, y = ((pos[d] + o) % RING[d] for d, o in zip(DIMS, offset))
    return (x * 2 + z) * 4 + y


def neighbour(pos, dim, step):
    moved = dict(pos)
    moved[dim] = (pos[dim] + step) % RING[dim]
    return device_at(moved)


def gather_kernel(own_ref, all_ref, send_sems, recv_sems, local_sem):
    pos = position()
    barrier = pltpu.get_barrier_semaphore()
    peers = [neighbour(pos, d, s) for d, s in (("x", 1), ("x", -1), ("y", 1), ("y", -1), ("z", 1))]
    for peer in peers:
        pl.semaphore_signal(barrier, inc=1, device_id=peer, device_id_type=MESH)
    pl.semaphore_wait(barrier, len(peers))
    mine = pltpu.make_async_copy(own_ref, all_ref.at[col_at(pos, (0, 0, 0))], local_sem)
    mine.start()
    started = []
    for key, offset, start, count, sends in PLAN:
        slot = all_ref.at[col_at(pos, offset)]
        if key is not None:
            view = slot.at[pl.ds(start, count)]
            pltpu.make_async_remote_copy(
                src_ref=view, dst_ref=view,
                send_sem=send_sems.at[COPY_IDS[key]], recv_sem=recv_sems.at[COPY_IDS[key]],
                device_id=peers[0], device_id_type=MESH,
            ).wait_recv()
        for dim, step, s0, n, target in sends:
            source = (own_ref if key is None else slot).at[pl.ds(s0, n)]
            copy = pltpu.make_async_remote_copy(
                src_ref=source, dst_ref=slot.at[pl.ds(s0, n)],
                send_sem=send_sems.at[COPY_IDS[target]], recv_sem=recv_sems.at[COPY_IDS[target]],
                device_id=neighbour(pos, dim, step), device_id_type=MESH,
            )
            copy.start()
            started.append(copy)
    for copy in started:
        copy.wait_send()
    mine.wait()


def gather_all(own):
    rows, rhs = own.shape
    return pl.pallas_call(
        gather_kernel,
        out_shape=jax.ShapeDtypeStruct((32, rows, rhs), own.dtype),
        in_specs=[pl.BlockSpec(memory_space=pl.ANY)],
        out_specs=pl.BlockSpec(memory_space=pl.ANY),
        scratch_shapes=[
            pltpu.SemaphoreType.DMA((COPIES,)), pltpu.SemaphoreType.DMA((COPIES,)), pltpu.SemaphoreType.DMA,
        ],
        compiler_params=pltpu.CompilerParams(collective_id=0, has_side_effects=True),
        name="gather_all",
    )(own)


def product_kernel(cols_ref, fresh_ref, ptrs_ref, values_ref, all_ref, out_ref, pieces, running, sems):
    slots = pieces.shape[0]
    size = pieces.shape[1]

    def fetch(e):
        return pltpu.make_async_copy(all_ref.at[cols_ref[e]], pieces.at[e], sems.at[e])

    @pl.loop(0, slots)
    def _(e):
        fetch(e).start()

    def pair(t, acc):
        e = t * 2
        fetch(e).wait()
        fetch(e + 1).wait()
        both = values_ref[:, pl.ds(pl.multiple_of(e * size, 2 * size), 2 * size)]
        zero = jnp.zeros((size, pieces.shape[2]), pieces.dtype)
        right = jnp.concatenate(
            [jnp.concatenate([pieces[e], zero], axis=1), jnp.concatenate([zero, pieces[e + 1]], axis=1)], axis=0
        )
        product = jnp.dot(both, right, preferred_element_type=jnp.float32)
        width = pieces.shape[2]
        for k in range(2):
            acc = jnp.where(fresh_ref[e + k] == 1, 0.0, acc) + product[:, k * width:(k + 1) * width]
            running[e + k] = acc
        return acc

    lax.fori_loop(0, slots // 2, pair, jnp.zeros(running.shape[1:], jnp.float32), unroll=4)

    @pl.loop(0, out_ref.shape[0])
    def _(l):
        end = ptrs_ref[l + 1]
        keep = end > ptrs_ref[l]
        value = running[jnp.maximum(end - 1, 0)]
        out_ref[l] = jnp.where(keep, value, 0.0)


def block_products(cols, fresh, ptrs, values, gathered):
    size = values.shape[0]
    slots = cols.shape[0]
    rhs = gathered.shape[-1]
    pieces = gathered.reshape(-1, size, rhs)
    tile_rows = ptrs.shape[0] - 1
    return pl.pallas_call(
        product_kernel,
        out_shape=jax.ShapeDtypeStruct((tile_rows, size, rhs), jnp.float32),
        in_specs=[pl.BlockSpec(memory_space=pltpu.SMEM)] * 3
        + [pl.BlockSpec(memory_space=pltpu.VMEM), pl.BlockSpec(memory_space=pl.ANY)],
        out_specs=pl.BlockSpec(memory_space=pltpu.VMEM),
        scratch_shapes=[
            pltpu.VMEM((slots, size, rhs), jnp.bfloat16),
            pltpu.VMEM((slots, size, rhs), jnp.float32),
            pltpu.SemaphoreType.DMA((slots,)),
        ],
        name="block_products",
    )(cols, fresh, ptrs, values, pieces)


CHUNKS = 4


def reduce_kernel(part_ref, smoothed_ref, residual_ref, applied_ref, stats_ref,
                  from_core, far, relay, landed, mine, others,
                  core_send, core_recv, relay_send, relay_recv, far_send, far_recv, sum_send, sum_recv):
    pos = position()
    h, core, z = pos["h"], pos["core"], pos["z"]
    height = h * 2 + z

    def along_z(step):
        moved = dict(pos)
        level = (height + step) % 4
        moved["h"], moved["z"] = level // 2, level % 2
        return device_at(moved)

    partner = device_at({**pos, "core": 1 - core})
    groups = [
        [partner],
        [along_z(s) for s in (1, 2, 3)],
        [neighbour(pos, "x", s) for s in (1, 2, 3)],
        [neighbour(pos, "y", s) for s in (1, 2, 3)],
    ]
    barrier = pltpu.get_barrier_semaphore()
    peers = [p for g in groups for p in g]
    for peer in peers:
        pl.semaphore_signal(barrier, inc=1, device_id=peer, device_id_type=MESH)
    pl.semaphore_wait(barrier, len(peers))

    swaps = []
    for k, level in enumerate((1 - h, h)):
        copy = pltpu.make_async_remote_copy(
            src_ref=part_ref.at[level * 2 + 1 - core], dst_ref=from_core.at[k],
            send_sem=core_send.at[k], recv_sem=core_recv.at[k], device_id=partner, device_id_type=MESH,
        )
        copy.start()
        swaps.append(copy)
    rows = part_ref.shape[1]
    step_rows = rows // CHUNKS
    swaps[0].wait_recv()
    order = [c for pair in zip(range(CHUNKS // 2), range(CHUNKS // 2, CHUNKS)) for c in pair]
    hops = {}
    for c in order:
        span = pl.ds(c * step_rows, step_rows)
        far[c] = part_ref[(1 - h) * 2 + core, span, :] + from_core[0, span, :]
    for c in order:
        direction = 1 if c < CHUNKS // 2 else 3
        hops[c] = pltpu.make_async_remote_copy(
            src_ref=far.at[c], dst_ref=relay.at[c],
            send_sem=relay_send.at[c], recv_sem=relay_recv.at[c],
            device_id=along_z(direction), device_id_type=MESH,
        )
        hops[c].start()
    ends = {}
    for c in order:
        direction = 1 if c < CHUNKS // 2 else 3
        hops[c].wait_recv()
        ends[c] = pltpu.make_async_remote_copy(
            src_ref=relay.at[c], dst_ref=landed.at[c],
            send_sem=far_send.at[c], recv_sem=far_recv.at[c],
            device_id=along_z(direction), device_id_type=MESH,
        )
        ends[c].start()
    gamma = jnp.sum(residual_ref[...] * smoothed_ref[...], axis=0, keepdims=True)
    swaps[1].wait_recv()
    delta = jnp.zeros_like(gamma)
    for c in order:
        span = pl.ds(c * step_rows, step_rows)
        ends[c].wait_recv()
        value = part_ref[h * 2 + core, span, :] + from_core[1, span, :] + landed[c]
        applied_ref[span, :] = value
        delta = delta + jnp.sum(smoothed_ref[span, :] * value, axis=0, keepdims=True)
    total = jnp.concatenate([gamma, delta, jnp.zeros((6, gamma.shape[1]), jnp.float32)], axis=0)
    sums = []
    base = 0
    for g, group in enumerate(groups):
        mine[g] = total
        batch = []
        for k, peer in enumerate(group):
            copy = pltpu.make_async_remote_copy(
                src_ref=mine.at[g], dst_ref=others.at[base + k],
                send_sem=sum_send.at[base + k], recv_sem=sum_recv.at[base + k],
                device_id=peer, device_id_type=MESH,
            )
            copy.start()
            batch.append(copy)
        for k, copy in enumerate(batch):
            copy.wait_recv()
            total = total + others[base + k]
        sums += batch
        base += len(group)
    stats_ref[...] = total
    for copy in swaps + list(hops.values()) + list(ends.values()) + sums:
        copy.wait_send()


def reduce_all(partial, smoothed, residual):
    rows, rhs = smoothed.shape
    dma = pltpu.SemaphoreType.DMA
    chunk = (CHUNKS, rows // CHUNKS, rhs)
    return pl.pallas_call(
        reduce_kernel,
        out_shape=(
            jax.ShapeDtypeStruct((rows, rhs), jnp.float32),
            jax.ShapeDtypeStruct((8, rhs), jnp.float32),
        ),
        in_specs=[pl.BlockSpec(memory_space=pltpu.VMEM)] * 3,
        out_specs=(pl.BlockSpec(memory_space=pltpu.VMEM),) * 2,
        scratch_shapes=[
            pltpu.VMEM((2, rows, rhs), jnp.float32),
            pltpu.VMEM(chunk, jnp.float32),
            pltpu.VMEM(chunk, jnp.float32),
            pltpu.VMEM(chunk, jnp.float32),
            pltpu.VMEM((4, 8, rhs), jnp.float32),
            pltpu.VMEM((10, 8, rhs), jnp.float32),
            dma((2,)), dma((2,)), dma((CHUNKS,)), dma((CHUNKS,)), dma((CHUNKS,)), dma((CHUNKS,)),
            dma((10,)), dma((10,)),
        ],
        compiler_params=pltpu.CompilerParams(collective_id=1, has_side_effects=True),
        name="reduce_all",
    )(partial, smoothed, residual)


def per_device(right_side, block_values, block_cols, row_ptrs, precond):
    slot_count = block_cols.shape[0]
    seg_rows, rhs_count = right_side.shape
    slot_index = jnp.arange(slot_count, dtype=jnp.int32)
    fresh = jnp.any(slot_index[:, None] == row_ptrs[None, :-1], axis=1).astype(jnp.int32)
    solution = jnp.zeros_like(right_side)
    residual = right_side
    for iteration in range(ITERS):
        half_step = jnp.dot(
            precond, residual, precision=lax.Precision.HIGHEST, preferred_element_type=jnp.float32
        )
        smoothed = lax.dot_general(
            precond, half_step, (((0,), (0,)), ((), ())),
            precision=lax.Precision.HIGHEST, preferred_element_type=jnp.float32,
        )
        gathered = gather_all(smoothed.astype(jnp.bfloat16))
        partial = block_products(block_cols, fresh, row_ptrs, block_values, gathered)
        applied, stats = reduce_all(partial.reshape(4, seg_rows, rhs_count), smoothed, residual)
        gamma_now, delta_now = stats[0], stats[1]
        if iteration == 0:
            alpha_now = gamma_now / delta_now
            direction = smoothed
            image_vec = applied
        else:
            beta_now = gamma_now / gamma_prev
            alpha_now = gamma_now / (delta_now - beta_now * gamma_now / alpha_prev)
            direction = smoothed + beta_now * direction
            image_vec = applied + beta_now * image_vec
        solution = solution + alpha_now * direction
        residual = residual - alpha_now * image_vec
        gamma_prev = gamma_now
        alpha_prev = alpha_now
    return (solution, residual)


def solution(mesh):
    return jax.shard_map(
        per_device,
        mesh=mesh,
        in_specs=(
            P(("row", "col"), None),
            P(None, ("row", "col")),
            P(("row", "col")),
            P(("row", "col")),
            P(("row", "col"), None),
        ),
        out_specs=(P(("row", "col"), None), P(("row", "col"), None)),
        check_vma=False,
    )
```

```python
import functools
import heapq

import jax
import jax.numpy as jnp
from jax import lax
from jax.experimental import pallas as pl
from jax.experimental.pallas import tpu as pltpu
from jax.sharding import PartitionSpec as P

MESH = pl.DeviceIdType.MESH
RING = {"x": 4, "z": 2, "y": 4}
DIMS = ("x", "z", "y")
PARTS = (
    (("z", "y", "x"), 0, 352),
    (("z", "x", "y"), 352, 352),
    (("y", "x", "z"), 704, 160),
    (("x", "y", "z"), 864, 160),
)
LINK_RATE = 46e3 / 256
HOP = 1.7
STRIPS = 4
GROUP = 16


def shifted(offset, dim, step):
    pos = DIMS.index(dim)
    changed = list(offset)
    changed[pos] = (changed[pos] + step) % RING[dim]
    return tuple(changed)


def sends_of(part, offset, stage):
    order, start, count = PARTS[part]
    half = count // 2
    out = []
    if stage >= 0 and order[stage] != "z":
        dim = order[stage]
        value = offset[DIMS.index(dim)]
        if value == 3:
            out.append((dim, 1, start, half, (part, shifted(offset, dim, -1), "p")))
        if value == 1:
            out.append((dim, -1, start + half, half, (part, shifted(offset, dim, 1), "m")))
    for later in range(stage + 1, 3):
        dim = order[later]
        out.append((dim, 1, start, count, (part, shifted(offset, dim, -1), "f")))
        if dim != "z":
            out.append((dim, -1, start, count, (part, shifted(offset, dim, 1), "f")))
    return out


def last_stage(part, offset):
    order = PARTS[part][0]
    return max(j for j in range(3) if offset[DIMS.index(order[j])] != 0)


def gather_plan():
    heap, free, ids, plan = [], {}, {}, []

    def issue(now, offset, sends):
        for dim, step, start, count, key in sends:
            link = (dim, step)
            free[link] = max(free.get(link, 0.0), now) + count / LINK_RATE
            ids[key] = len(ids)
            heapq.heappush(heap, (free[link] + HOP, ids[key], key, start, count))

    first = []
    for part in range(len(PARTS)):
        first += [(j, s) for j, s in enumerate(sends_of(part, (0, 0, 0), -1))]
    first = [s for _, s in sorted(first, key=lambda item: item[0])]
    issue(0.0, (0, 0, 0), first)
    plan.append((None, (0, 0, 0), 0, 0, first))
    halves = set()
    while heap:
        now, _, key, start, count = heapq.heappop(heap)
        part, offset, kind = key
        stage = last_stage(part, offset)
        sends = []
        if kind == "f":
            sends = sends_of(part, offset, stage)
        elif (part, offset) in halves:
            sends = sends_of(part, offset, stage)
        else:
            halves.add((part, offset))
        issue(now, offset, sends)
        plan.append((key, offset, start, count, sends))
    return plan, ids


PLAN, COPY_IDS = gather_plan()
COPIES = len(COPY_IDS)


def position():
    row = lax.axis_index("row")
    col = lax.axis_index("col")
    return {
        "h": row // 2, "core": row % 2,
        "x": col // 8, "z": (col // 4) % 2, "y": col % 4,
    }


def device_at(pos):
    return (pos["h"] * 2 + pos["core"], (pos["x"] * 2 + pos["z"]) * 4 + pos["y"])


def col_at(pos, offset):
    x, z, y = ((pos[d] + o) % RING[d] for d, o in zip(DIMS, offset))
    return (x * 2 + z) * 4 + y


def split(value):
    high = value.astype(jnp.bfloat16)
    return high, (value - high.astype(jnp.float32)).astype(jnp.bfloat16)


def wide_dot(a, b):
    def dot(p, q):
        return jnp.dot(p, q, preferred_element_type=jnp.float32)
    return dot(a[0], b[0]) + (dot(a[0], b[1]) + dot(a[1], b[0]))


def factor_copies(factor_ref, factor, sems):
    rows = factor.shape[0]
    tall = rows // STRIPS
    return [
        pltpu.make_async_copy(
            factor_ref.at[pl.ds(i * tall, tall), pl.ds(0, (i + 1) * tall)],
            factor.at[pl.ds(i * tall, tall), pl.ds(0, (i + 1) * tall)],
            sems.at[i],
        )
        for i in range(STRIPS)
    ]


def precondition_strip(i, factor, vector, flipped):
    tall = factor.shape[0] // STRIPS
    wide = (i + 1) * tall
    strip = split(factor[pl.ds(i * tall, tall), pl.ds(0, wide)])
    inner = wide_dot(strip, (vector[0, pl.ds(0, wide), :], vector[1, pl.ds(0, wide), :]))
    outer = wide_dot(split(inner.T), strip)
    if i == STRIPS - 1:
        flipped[:, pl.ds(0, wide)] = outer
    else:
        flipped[:, pl.ds(0, wide)] = flipped[:, pl.ds(0, wide)] + outer


def precondition_kernel(factor_ref, vector_ref, out_ref, half_ref, factor, vector, flipped, sems):
    copies = factor_copies(factor_ref, factor, sems)
    for copy in reversed(copies):
        copy.start()
    vector[0], vector[1] = split(vector_ref[...])
    for i in reversed(range(STRIPS)):
        copies[i].wait()
        precondition_strip(i, factor, vector, flipped)
    result = flipped[...].T
    out_ref[...] = result
    half_ref[...] = result.astype(jnp.bfloat16)


def precondition(factor, vector):
    rows, rhs = vector.shape
    return pl.pallas_call(
        precondition_kernel,
        out_shape=(
            jax.ShapeDtypeStruct((rows, rhs), jnp.float32),
            jax.ShapeDtypeStruct((rows, rhs), jnp.bfloat16),
        ),
        in_specs=[pl.BlockSpec(memory_space=pl.ANY), pl.BlockSpec(memory_space=pltpu.VMEM)],
        out_specs=(pl.BlockSpec(memory_space=pltpu.VMEM),) * 2,
        scratch_shapes=[
            pltpu.VMEM((rows, rows), jnp.float32),
            pltpu.VMEM((2, rows, rhs), jnp.bfloat16),
            pltpu.VMEM((rhs, rows), jnp.float32),
            pltpu.SemaphoreType.DMA((STRIPS,)),
        ],
        name="precondition",
    )(factor, vector)


def neighbour(pos, dim, step):
    moved = dict(pos)
    moved[dim] = (pos[dim] + step) % RING[dim]
    return device_at(moved)


def gather_kernel(own_ref, all_ref, send_sems, recv_sems, local_sem):
    pos = position()
    barrier = pltpu.get_barrier_semaphore()
    peers = [neighbour(pos, d, s) for d, s in (("x", 1), ("x", -1), ("y", 1), ("y", -1), ("z", 1))]
    for peer in peers:
        pl.semaphore_signal(barrier, inc=1, device_id=peer, device_id_type=MESH)
    pl.semaphore_wait(barrier, len(peers))
    mine = pltpu.make_async_copy(own_ref, all_ref.at[col_at(pos, (0, 0, 0))], local_sem)
    mine.start()
    started = []
    for key, offset, start, count, sends in PLAN:
        slot = all_ref.at[col_at(pos, offset)]
        if key is not None:
            view = slot.at[pl.ds(start, count)]
            pltpu.make_async_remote_copy(
                src_ref=view, dst_ref=view,
                send_sem=send_sems.at[COPY_IDS[key]], recv_sem=recv_sems.at[COPY_IDS[key]],
                device_id=peers[0], device_id_type=MESH,
            ).wait_recv()
        for dim, step, s0, n, target in sends:
            source = (own_ref if key is None else slot).at[pl.ds(s0, n)]
            copy = pltpu.make_async_remote_copy(
                src_ref=source, dst_ref=slot.at[pl.ds(s0, n)],
                send_sem=send_sems.at[COPY_IDS[target]], recv_sem=recv_sems.at[COPY_IDS[target]],
                device_id=neighbour(pos, dim, step), device_id_type=MESH,
            )
            copy.start()
            started.append(copy)
    for copy in started:
        copy.wait_send()
    mine.wait()


def gather_all(own):
    rows, rhs = own.shape
    return pl.pallas_call(
        gather_kernel,
        out_shape=jax.ShapeDtypeStruct((32, rows, rhs), own.dtype),
        in_specs=[pl.BlockSpec(memory_space=pl.ANY)],
        out_specs=pl.BlockSpec(memory_space=pl.ANY),
        scratch_shapes=[
            pltpu.SemaphoreType.DMA((COPIES,)), pltpu.SemaphoreType.DMA((COPIES,)), pltpu.SemaphoreType.DMA,
        ],
        compiler_params=pltpu.CompilerParams(collective_id=0, has_side_effects=True),
        name="gather_all",
    )(own)


def product_kernel(cols_ref, fresh_ref, ptrs_ref, values_ref, all_ref, out_ref, pieces, running, sems):
    slots, size, width = pieces.shape

    def fetch(e):
        return pltpu.make_async_copy(all_ref.at[cols_ref[e]], pieces.at[e], sems.at[e])

    def begin(e, carry):
        fetch(e).start()
        return carry

    lax.fori_loop(0, slots, begin, 0, unroll=8)
    zero = jnp.zeros((size, width), pieces.dtype)

    def group(g, acc):
        first = g * GROUP
        for k in range(GROUP):
            fetch(first + k).wait()
        for k in range(0, GROUP, 2):
            e = first + k
            both = values_ref[:, pl.ds(pl.multiple_of(e * size, 2 * size), 2 * size)]
            right = jnp.concatenate(
                [jnp.concatenate([pieces[e], zero], axis=1), jnp.concatenate([zero, pieces[e + 1]], axis=1)],
                axis=0,
            )
            product = jnp.dot(both, right, preferred_element_type=jnp.float32)
            for j in range(2):
                acc = jnp.where(fresh_ref[e + j] == 1, 0.0, acc) + product[:, j * width:(j + 1) * width]
                running[e + j] = acc
        return acc

    lax.fori_loop(0, slots // GROUP, group, jnp.zeros((size, width), jnp.float32))

    def finish(l, carry):
        end = ptrs_ref[l + 1]
        value = running[jnp.maximum(end - 1, 0)]
        out_ref[l] = jnp.where(end > ptrs_ref[l], value, 0.0)
        return carry

    lax.fori_loop(0, out_ref.shape[0], finish, 0, unroll=8)


def block_products(cols, fresh, ptrs, values, gathered):
    size = values.shape[0]
    slots = cols.shape[0]
    rhs = gathered.shape[-1]
    pieces = gathered.reshape(-1, size, rhs)
    tile_rows = ptrs.shape[0] - 1
    return pl.pallas_call(
        product_kernel,
        out_shape=jax.ShapeDtypeStruct((tile_rows, size, rhs), jnp.float32),
        in_specs=[pl.BlockSpec(memory_space=pltpu.SMEM)] * 3
        + [pl.BlockSpec(memory_space=pltpu.VMEM), pl.BlockSpec(memory_space=pl.ANY)],
        out_specs=pl.BlockSpec(memory_space=pltpu.VMEM),
        scratch_shapes=[
            pltpu.VMEM((slots, size, rhs), jnp.bfloat16),
            pltpu.VMEM((slots, size, rhs), jnp.float32),
            pltpu.SemaphoreType.DMA((slots,)),
        ],
        name="block_products",
    )(cols, fresh, ptrs, values, pieces)


CHUNKS = 8
HALF_CHUNKS = CHUNKS // 2


def reduce_kernel(last, *refs):
    if last:
        part_ref, smoothed_ref, residual_ref, applied_ref, stats_ref = refs[:5]
        scratch = refs[5:]
    else:
        part_ref, smoothed_ref, residual_ref, factor_ref = refs[:4]
        applied_ref, stats_ref, next_ref, half_ref, update_ref = refs[4:9]
        factor, vector, flipped, factor_sems = refs[9:13]
        scratch = refs[13:]
    (from_core, far, relay, landed, mine, others, core_send, core_recv, near_sems,
     relay_send, relay_recv, far_send, far_recv, sum_send, sum_recv) = scratch
    pos = position()
    h, core = pos["h"], pos["core"]
    height = h * 2 + pos["z"]

    def along_z(step, other=0):
        level = (height + step) % 4
        return device_at({**pos, "h": level // 2, "z": level % 2, "core": (core + other) % 2})

    partner = along_z(0, 1)
    groups = [
        [along_z(s, o) for s in range(4) for o in range(2) if s or o],
        [
            device_at({**pos, "x": (pos["x"] + i) % 4, "y": (pos["y"] + j) % 4})
            for i in range(4) for j in range(4) if i or j
        ],
    ]
    barrier = pltpu.get_barrier_semaphore()
    peers = [p for g in groups for p in g]
    for peer in peers:
        pl.semaphore_signal(barrier, inc=1, device_id=peer, device_id_type=MESH)
    if not last:
        factor_loads = factor_copies(factor_ref, factor, factor_sems)
        for copy in reversed(factor_loads):
            copy.start()
    pl.semaphore_wait(barrier, len(peers))

    def send(source, target, send_sem, recv_sem, device):
        copy = pltpu.make_async_remote_copy(
            src_ref=source, dst_ref=target, send_sem=send_sem, recv_sem=recv_sem,
            device_id=device, device_id_type=MESH,
        )
        copy.start()
        return copy

    rows = part_ref.shape[1]
    step_rows = rows // CHUNKS
    spans = [pl.ds(c * step_rows, step_rows) for c in range(CHUNKS)]
    order = [c for both in zip(range(HALF_CHUNKS), range(HALF_CHUNKS, CHUNKS)) for c in both]
    ways = [along_z(1 if c < HALF_CHUNKS else 3) for c in range(CHUNKS)]
    swaps = {
        c: send(part_ref.at[(1 - h) * 2 + 1 - core, spans[c]], from_core.at[0, spans[c]],
                core_send.at[c], core_recv.at[c], partner)
        for c in order
    }
    near = send(part_ref.at[h * 2 + 1 - core], from_core.at[1], near_sems.at[0], near_sems.at[1], partner)
    hops, ends = {}, {}
    ready = []
    for c in order + [None]:
        if c is not None:
            swaps[c].wait_recv()
            total = part_ref[(1 - h) * 2 + core, spans[c], :] + from_core[0, spans[c], :]
            far[c] = total.astype(far.dtype)
            ready.append(c)
        if c is None or len(ready) > 1:
            k = ready.pop(0)
            hops[k] = send(far.at[k], relay.at[k], relay_send.at[k], relay_recv.at[k], ways[k])
    for c in order:
        hops[c].wait_recv()
        ends[c] = send(relay.at[c], landed.at[c], far_send.at[c], far_recv.at[c], ways[c])
    gamma = jnp.sum(residual_ref[...] * smoothed_ref[...], axis=0, keepdims=True)
    near.wait_recv()
    delta = jnp.zeros_like(gamma)
    for c in order:
        span = spans[c]
        local = part_ref[h * 2 + core, span, :] + from_core[1, span, :]
        ends[c].wait_recv()
        value = local + landed[c].astype(jnp.float32)
        applied_ref[span, :] = value
        if not last:
            vector[0, span, :], vector[1, span, :] = split(value)
        delta = delta + jnp.sum(smoothed_ref[span, :] * value, axis=0, keepdims=True)
    total = jnp.concatenate([gamma, delta, jnp.zeros((6, gamma.shape[1]), jnp.float32)], axis=0)
    sums = []
    base = 0
    strips = list(reversed(range(STRIPS)))
    for g, group in enumerate(groups):
        mine[g] = total
        batch = [
            send(mine.at[g], others.at[base + k], sum_send.at[base + k], sum_recv.at[base + k], peer)
            for k, peer in enumerate(group)
        ]
        if not last:
            for i in strips[:1] if g == 0 else strips[1:]:
                factor_loads[i].wait()
                precondition_strip(i, factor, vector, flipped)
        for k, copy in enumerate(batch):
            copy.wait_recv()
            total = total + others[base + k]
        sums += batch
        base += len(group)
    stats_ref[...] = total
    if not last:
        alpha = total[0:1] / total[1:2]
        following = smoothed_ref[...] - alpha * flipped[...].T
        next_ref[...] = following
        half_ref[...] = following.astype(jnp.bfloat16)
        update_ref[...] = residual_ref[...] - alpha * applied_ref[...]
    for copy in list(swaps.values()) + [near] + list(hops.values()) + list(ends.values()) + sums:
        copy.wait_send()


def reduce_all(partial, smoothed, residual, factor=None):
    last = factor is None
    rows, rhs = smoothed.shape
    dma = pltpu.SemaphoreType.DMA
    chunk = pltpu.VMEM((CHUNKS, rows // CHUNKS, rhs), jnp.bfloat16)
    whole = jax.ShapeDtypeStruct((rows, rhs), jnp.float32)
    outs = [whole, jax.ShapeDtypeStruct((8, rhs), jnp.float32)]
    operands = [partial, smoothed, residual]
    specs = [pl.BlockSpec(memory_space=pltpu.VMEM)] * 3
    scratch = []
    if not last:
        outs += [whole, jax.ShapeDtypeStruct((rows, rhs), jnp.bfloat16), whole]
        operands.append(factor)
        specs.append(pl.BlockSpec(memory_space=pl.ANY))
        scratch = [
            pltpu.VMEM((rows, rows), jnp.float32),
            pltpu.VMEM((2, rows, rhs), jnp.bfloat16),
            pltpu.VMEM((rhs, rows), jnp.float32),
            dma((STRIPS,)),
        ]
    scratch += [
        pltpu.VMEM((2, rows, rhs), jnp.float32), chunk, chunk, chunk,
        pltpu.VMEM((2, 8, rhs), jnp.float32), pltpu.VMEM((22, 8, rhs), jnp.float32),
        dma((CHUNKS,)), dma((CHUNKS,)), dma((2,)),
        dma((CHUNKS,)), dma((CHUNKS,)), dma((CHUNKS,)), dma((CHUNKS,)),
        dma((22,)), dma((22,)),
    ]
    return pl.pallas_call(
        functools.partial(reduce_kernel, last),
        out_shape=tuple(outs),
        in_specs=specs,
        out_specs=(pl.BlockSpec(memory_space=pltpu.VMEM),) * len(outs),
        scratch_shapes=scratch,
        compiler_params=pltpu.CompilerParams(collective_id=2 if last else 1, has_side_effects=True),
        name="reduce_last" if last else "reduce_first",
    )(*operands)


def per_device(right_side, block_values, block_cols, row_ptrs, precond):
    slot_count = block_cols.shape[0]
    seg_rows, rhs_count = right_side.shape
    slot_index = jnp.arange(slot_count, dtype=jnp.int32)
    fresh = jnp.any(slot_index[:, None] == row_ptrs[None, :-1], axis=1).astype(jnp.int32)

    def apply(half):
        partial = block_products(block_cols, fresh, row_ptrs, block_values, gather_all(half))
        return partial.reshape(4, seg_rows, rhs_count)

    first, half = precondition(precond, right_side)
    image, stats, second, half, residual = reduce_all(apply(half), first, right_side, precond)
    applied, last_stats = reduce_all(apply(half), second, residual)
    gamma_prev, gamma_now = stats[0], last_stats[0]
    alpha_prev = gamma_prev / stats[1]
    beta = gamma_now / gamma_prev
    alpha = gamma_now / (last_stats[1] - beta * gamma_now / alpha_prev)
    solution = alpha_prev * first + alpha * (second + beta * first)
    residual = residual - alpha * (applied + beta * image)
    return (solution, residual)


def solution(mesh):
    return jax.shard_map(
        per_device,
        mesh=mesh,
        in_specs=(
            P(("row", "col"), None),
            P(None, ("row", "col")),
            P(("row", "col")),
            P(("row", "col")),
            P(("row", "col"), None),
        ),
        out_specs=(P(("row", "col"), None), P(("row", "col"), None)),
        check_vma=False,
    )
```
